32 devices in a mesh: gx: 4 (over y, x), gy: 8 (over z, core).
Axes of the slice: x: 2, y: 2, z: 4, core: 2. Of those that a mesh axis runs over, the one named last changes fastest.
Arguments:
- thermal_field: float32 [192, 192, 128], P('gx', 'gy'), may hold values from -6 to 6
- generator_keys: int32 [6], replicated, may hold values from 0 to 1048575
- slab_top_offset: int32 [1], replicated, may hold values from 0 to 2047
Outputs:
- factor_x: float32 [192, 64], P('gx')
- factor_y: float32 [192, 64], P('gy')
- factor_z: float32 [128, 64], replicated
- core: float32 [128, 128, 128], P('gx', 'gy')
The draws below stay inside these ranges and needn't reach their ends.
All inputs are finite; a program needn't handle non-finite values.
Results may differ from the reference program's by a relative error of at most 0.000071.
Values sent between devices are 32-bit elements; how exact they have to be, the bound alone decides.
A program may use at most 64 MiB of HBM per device.

```python
import math
import jax
import jax.numpy as jnp
from jax import lax

VERTICAL_COUNT = 128
RANK = 64
TARGET_RANK = 128
ZONAL_COUNT = 192
MERIDIONAL_COUNT = 192


def place_ends(entries, key, smallest, top_value):
    index_at = [jax.random.randint(jax.random.fold_in(key, axis), (), 0, length) for axis, length in enumerate(entries.shape)]
    widest = entries.shape.index(max(entries.shape))
    beside = index_at[:widest] + [(index_at[widest] + 1) % entries.shape[widest]] + index_at[widest + 1:]
    return entries.at[tuple(index_at)].set(smallest).at[tuple(beside)].set(top_value)


def levels(stream_key, shape, cuts, low, largest):
    def one(axis_at, parts):
        draws = jax.random.uniform(jax.random.fold_in(jax.random.fold_in(stream_key, 6), axis_at), (parts,), jnp.float32, low / len(cuts), largest / len(cuts))
        return jnp.repeat(jnp.exp(draws), shape[axis_at] // parts).reshape((-1,) + (1,) * (len(shape) - axis_at - 1))

    level = one(*cuts[0])
    for cut in cuts[1:]:
        level = level * one(*cut)
    return level


def gaussian(stream_key, dims, scale, bound, split=(), kind=jnp.bfloat16):
    level = levels(stream_key, dims, split, -0.22, 0.18) if split else 1.0
    drawn = jax.random.normal(stream_key, dims, jnp.float32) * scale * level
    return jnp.minimum(jnp.maximum(drawn, -bound), bound).astype(kind)


def setup_inputs(seed: int = 0) -> dict:
    keys = jax.random.split(jax.random.key(seed), 4)
    thermal_field = gaussian(keys[0], (ZONAL_COUNT, MERIDIONAL_COUNT, VERTICAL_COUNT), 1.0, 6.0, ((0, 4), (1, 8)), jnp.float32)
    generator_keys = place_ends(jax.random.randint(keys[1], (6,), 0, 1048576), jax.random.fold_in(keys[1], 1), 0, 1048575).astype(jnp.int32)
    slab_top_offset = jax.random.randint(keys[2], (1,), 0, 2048).astype(jnp.int32)
    return {"thermal_field": thermal_field, "generator_keys": generator_keys, "slab_top_offset": slab_top_offset}


def random_signs(seed_value, cell_index, column_index):
    hashed = cell_index * 73856093 + column_index * 19349663 + seed_value * 83492791
    hashed = jnp.bitwise_xor(hashed, lax.shift_right_logical(hashed, jnp.full_like(hashed, 15)))
    hashed = hashed * 668265261
    hashed = jnp.bitwise_xor(hashed, lax.shift_right_logical(hashed, jnp.full_like(hashed, 13)))
    parity = jnp.bitwise_and(lax.shift_right_logical(hashed, jnp.full_like(hashed, 7)), jnp.full_like(hashed, 1))
    return jnp.where(parity == 1, 1.0, -1.0).astype(jnp.float32)

def reference(thermal_field, generator_keys, slab_top_offset):
    exact_matmul_mode = lax.Precision.HIGHEST
    x_index = jnp.arange(ZONAL_COUNT, dtype=jnp.int32)[:, None]
    y_index = jnp.arange(MERIDIONAL_COUNT, dtype=jnp.int32)[:, None]
    z_index = (slab_top_offset[0] + jnp.arange(VERTICAL_COUNT, dtype=jnp.int32))[:, None]
    rank_cols = jnp.arange(RANK, dtype=jnp.int32)[None, :]
    core_cols = jnp.arange(TARGET_RANK, dtype=jnp.int32)[None, :]
    omega_x = random_signs(generator_keys[0], x_index, rank_cols)
    omega_y = random_signs(generator_keys[1], y_index, rank_cols)
    omega_z = random_signs(generator_keys[2], z_index, rank_cols)
    zonal_compressed = random_signs(generator_keys[3], x_index, core_cols)
    phi_y = random_signs(generator_keys[4], y_index, core_cols)
    phi_z = random_signs(generator_keys[5], z_index, core_cols)
    unrolled_grid = thermal_field.reshape(ZONAL_COUNT * MERIDIONAL_COUNT, VERTICAL_COUNT)
    reduced = jnp.dot(unrolled_grid, omega_z, precision=exact_matmul_mode).reshape(ZONAL_COUNT, MERIDIONAL_COUNT, RANK)
    factor_x = jnp.einsum('xyk,yk->xk', reduced, omega_y, precision=exact_matmul_mode) * (1.0 / math.sqrt(MERIDIONAL_COUNT * VERTICAL_COUNT))
    factor_y = jnp.einsum('xyk,xk->yk', reduced, omega_x, precision=exact_matmul_mode) * (1.0 / math.sqrt(ZONAL_COUNT * VERTICAL_COUNT))
    khatri = (omega_x[:, None, :] * omega_y[None, :, :]).reshape(ZONAL_COUNT * MERIDIONAL_COUNT, RANK)
    factor_z = jnp.einsum('pz,pk->zk', unrolled_grid, khatri, precision=exact_matmul_mode) * (1.0 / math.sqrt(ZONAL_COUNT * MERIDIONAL_COUNT))
    front_portion = jnp.dot(zonal_compressed.T, thermal_field.reshape(ZONAL_COUNT, MERIDIONAL_COUNT * VERTICAL_COUNT), precision=exact_matmul_mode).reshape(TARGET_RANK, MERIDIONAL_COUNT, VERTICAL_COUNT)
    second = jnp.einsum('ayz,yb->abz', front_portion, phi_y, precision=exact_matmul_mode)
    core = jnp.einsum('abz,zc->abc', second, phi_z, precision=exact_matmul_mode) * (1.0 / math.sqrt(ZONAL_COUNT * MERIDIONAL_COUNT * VERTICAL_COUNT))
    return (factor_x, factor_y, factor_z, core)
```

```python
import functools
import math

import jax
import jax.numpy as jnp
from jax import lax
from jax.experimental import pallas as pl
from jax.experimental.pallas import tpu as pltpu
from jax.sharding import PartitionSpec as P

RANK = 64
TARGET_RANK = 128


def random_signs(seed_value, cell_index, column_index):
    hashed = cell_index * 73856093 + column_index * 19349663 + seed_value * 83492791
    hashed = jnp.bitwise_xor(hashed, lax.shift_right_logical(hashed, jnp.full_like(hashed, 15)))
    hashed = hashed * 668265261
    hashed = jnp.bitwise_xor(hashed, lax.shift_right_logical(hashed, jnp.full_like(hashed, 13)))
    parity = jnp.bitwise_and(
        lax.shift_right_logical(hashed, jnp.full_like(hashed, 7)), jnp.full_like(hashed, 1)
    )
    return jnp.where(parity == 1, 1.0, -1.0).astype(jnp.float32)


def body(thermal_field, generator_keys, slab_top_offset):
    exact_matmul_mode = lax.Precision.HIGHEST
    front_length, back_length, vertical_layer = thermal_field.shape
    devices_first = lax.axis_size("gx")
    devices_second = lax.axis_size("gy")
    total_first = front_length * devices_first
    total_second = back_length * devices_second
    x_index = (lax.axis_index("gx") * front_length + jnp.arange(front_length, dtype=jnp.int32))[
        :, None
    ]
    y_index = (lax.axis_index("gy") * back_length + jnp.arange(back_length, dtype=jnp.int32))[
        :, None
    ]
    z_index = (slab_top_offset[0] + jnp.arange(vertical_layer, dtype=jnp.int32))[:, None]
    rank_cols = jnp.arange(RANK, dtype=jnp.int32)[None, :]
    core_cols = jnp.arange(TARGET_RANK, dtype=jnp.int32)[None, :]
    omega_x = random_signs(generator_keys[0], x_index, rank_cols)
    omega_y = random_signs(generator_keys[1], y_index, rank_cols)
    omega_z = random_signs(generator_keys[2], z_index, rank_cols)
    phi_xt = random_signs(generator_keys[3], x_index, core_cols).T
    phi_yt = random_signs(generator_keys[4], y_index, core_cols).T
    phi_z = random_signs(generator_keys[5], z_index, core_cols)
    unrolled_grid = thermal_field.reshape(front_length * back_length, vertical_layer)
    reduced = jnp.dot(unrolled_grid, omega_z, precision=exact_matmul_mode).reshape(
        front_length, back_length, RANK
    )
    partial_x = jnp.einsum("xyk,yk->xk", reduced, omega_y, precision=exact_matmul_mode)
    partial_y = jnp.einsum("xyk,xk->yk", reduced, omega_x, precision=exact_matmul_mode)
    khatri = (omega_x[:, None, :] * omega_y[None, :, :]).reshape(front_length * back_length, RANK)
    partial_z = jnp.einsum("pz,pk->zk", unrolled_grid, khatri, precision=exact_matmul_mode)
    summed_x, half_z = lax.psum((partial_x, partial_z), "gy")
    summed_y, summed_z = lax.psum((partial_y, half_z), "gx")
    factor_x = summed_x * (1.0 / math.sqrt(total_second * vertical_layer))
    factor_y = summed_y * (1.0 / math.sqrt(total_first * vertical_layer))
    factor_z = summed_z * (1.0 / math.sqrt(total_first * total_second))
    thermal_matrix = thermal_field.reshape(front_length, back_length * vertical_layer)
    chosen_entries = phi_xt
    reduced_first = lax.psum_scatter(
        jnp.dot(chosen_entries, thermal_matrix, precision=exact_matmul_mode),
        "gx",
        scatter_dimension=0,
        tiled=True,
    )
    reduced_first = reduced_first.reshape(-1, back_length, vertical_layer)
    chosen_entries = phi_yt
    middle = jnp.einsum("by,ayz->baz", chosen_entries, reduced_first, precision=exact_matmul_mode)
    swapped = lax.psum_scatter(
        jnp.einsum("baz,zc->bac", middle, phi_z, precision=exact_matmul_mode),
        "gy",
        scatter_dimension=0,
        tiled=True,
    )
    core_block = jnp.transpose(swapped, (1, 0, 2))
    core = core_block * (1.0 / math.sqrt(total_first * total_second * vertical_layer))
    return (factor_x, factor_y, factor_z, core)


SUB = 8
LANES = 128
MESH_ID = pl.DeviceIdType.MESH


def signs(seed_value, cell_index, column_index):
    hashed = cell_index * 73856093 + column_index * 19349663 + seed_value * 83492791
    hashed = hashed ^ lax.shift_right_logical(hashed, jnp.full_like(hashed, 15))
    hashed = hashed * 668265261
    hashed = hashed ^ lax.shift_right_logical(hashed, jnp.full_like(hashed, 13))
    return jnp.where((hashed & 128) != 0, 1.0, -1.0).astype(jnp.float32)


def iota(shape, axis):
    return lax.broadcasted_iota(jnp.int32, shape, axis)


def split(value):
    high = value.astype(jnp.bfloat16)
    low = (value - high.astype(jnp.float32)).astype(jnp.bfloat16)
    return high, low


def mm(left, right):
    return jnp.dot(left, right, preferred_element_type=jnp.float32)


def flip(index, bit):
    return index + bit - 2 * bit * ((index // bit) % 2)


def kernel(
    dims,
    keys, top, field,
    out_x, out_y, out_z, out_core,
    spread, landed, own, near, far_out, far_in, done_out, done_in, kron,
    small_out, small_in, small_sum, zsum_in, zx_out, zx_in, fy_out, fy_in,
    s1, r1, s2, r2, s3, r3, s4, r4, t1, u1, t2, u2, t3, u3, t4, u4,
):
    nx, ng, front, back, depth = dims
    nz = ng // 2
    blk_a = TARGET_RANK // nx
    chunks = blk_a // (2 * SUB)
    blk_b = TARGET_RANK // nz
    out_b = blk_b // 2
    ix = lax.axis_index("gx")
    ig = lax.axis_index("gy")
    iz, core = ig // 2, ig % 2

    def dev_x(d):
        r = ix
        for bit in (1, 2):
            if d & bit:
                r = flip(r, bit)
        return r

    def dev_g(d):
        r = ig
        for bit in (1, 2, 4):
            if d & bit:
                r = flip(r, bit)
        return r

    def copy(src, dst, send, recv, dx, dg):
        return pltpu.make_async_remote_copy(
            src_ref=src, dst_ref=dst, send_sem=send, recv_sem=recv,
            device_id=(dev_x(dx), dev_g(dg)), device_id_type=MESH_ID,
        )

    partners = [(dx, dc) for dx in range(nx) for dc in range(2) if dx or dc]
    partners += [(0, dg) for dg in range(2, ng)]
    barrier = pltpu.get_barrier_semaphore()
    for dx, dg in partners:
        pl.semaphore_signal(
            barrier, inc=1, device_id=(dev_x(dx), dev_g(dg)), device_id_type=MESH_ID
        )

    x0 = ix * front
    y0 = ig * back
    z0 = top[0]

    rows = TARGET_RANK + RANK
    row = iota((rows, 2 * front), 0)
    lane = iota((rows, 2 * front), 1)
    cell = jnp.where(lane >= front, lane - front, lane) + x0
    is_core = row < TARGET_RANK
    left = signs(
        jnp.where(is_core, keys[3], keys[0]),
        cell,
        jnp.where(is_core, row, row - TARGET_RANK),
    ).astype(jnp.bfloat16)
    omega_yt = signs(keys[1], iota((RANK, back), 1) + y0, iota((RANK, back), 0))
    total_z = jnp.zeros((RANK, depth), jnp.float32)
    for y in range(back):
        high, low = split(field[pl.ds(y, front, stride=back), :])
        both = mm(left, jnp.concatenate([high, low], axis=0))
        spread[y] = both[:TARGET_RANK]
        total_z = total_z + both[TARGET_RANK:] * omega_yt[:, y : y + 1]

    pl.semaphore_wait(barrier, len(partners))

    pend = []
    first = []
    order = [d for d in ((3, 0), (3, 1), (1, 0), (2, 0), (1, 1), (2, 1), (0, 1))]
    for i in range(chunks):
        group = []
        for dx, dc in order:
            slot = dx * 2 + dc - 1
            start = dev_x(dx) * blk_a + i * 2 * SUB + (dev_g(dc) % 2) * SUB
            start = pl.multiple_of(start, SUB)
            group.append(copy(
                spread.at[:, pl.ds(start, SUB), :], landed.at[i, slot],
                s1.at[i, slot], r1.at[i, slot], dx, dc,
            ))
            group[-1].start()
        first.append(group)
        pend += group

    lane_z = iota((depth, LANES), 1)
    row_z = iota((depth, LANES), 0) + z0
    omega_z = signs(keys[2], row_z, lane_z).astype(jnp.bfloat16)
    high, low = split(field[...])
    reduced = (mm(high, omega_z) + mm(low, omega_z)).reshape(front, back, LANES)
    omega_y = signs(keys[1], iota((back, LANES), 0) + y0, iota((back, LANES), 1))
    part_y = jnp.zeros((back, LANES), jnp.float32)
    omega_x = signs(keys[0], iota((front, LANES), 0) + x0, iota((front, LANES), 1))
    part_x = jnp.sum(reduced * omega_y[None], axis=1)
    for x in range(front):
        part_y = part_y + reduced[x] * omega_x[x : x + 1]
    fy_out[...] = part_y
    per = front // ng
    kper = RANK // ng
    for d in range(ng):
        small_out[d, 0:kper] = total_z[d * kper : (d + 1) * kper]
        small_out[d, SUB : SUB + per] = part_x[d * per : (d + 1) * per]
    fy = []
    for d in range(1, nx):
        fy.append(copy(fy_out, fy_in.at[d - 1], t1.at[d - 1], u1.at[d - 1], d, 0))
        fy[-1].start()
    sm = []
    for d in range(1, ng):
        sm.append(copy(
            small_out.at[dev_g(d)], small_in.at[d - 1], t2.at[d - 1], u2.at[d - 1], 0, d
        ))
        sm[-1].start()
    pend += fy

    half = 2 * back * SUB
    for dst in range(2):
        for src in range(2):
            for dc in range(2):
                shape = (blk_b * SUB, back * SUB)
                row = iota(shape, 0)
                col = iota(shape, 1)
                chip_b = (flip(iz, 2) if dst else iz) * blk_b
                cell_y = dev_g(src * 2 + dc) * back
                value = signs(
                    keys[4],
                    lax.shift_right_logical(col, jnp.full_like(col, 3)) + cell_y,
                    lax.shift_right_logical(row, jnp.full_like(row, 3)) + chip_b,
                )
                value = jnp.where((row & 7) == (col & 7), value, 0.0)
                kron[src, dc, dst * blk_b * SUB : (dst + 1) * blk_b * SUB, :] = value.astype(
                    jnp.bfloat16
                )
    phi_z = signs(keys[5], row_z, lane_z).astype(jnp.bfloat16)

    def project(src, dc, block):
        high, low = split(block.reshape(back * SUB, depth))
        return mm(kron[src, dc], high) + mm(kron[src, dc], low)

    nearby = []
    sums = []
    for i in range(chunks):
        for c in first[i]:
            c.wait_recv()
        for dc in range(2):
            if dc:
                base = landed[i, 0]
            else:
                base = spread[:, pl.ds(
                    pl.multiple_of(ix * blk_a + i * 2 * SUB + core * SUB, SUB), SUB), :]
            for dx in range(1, nx):
                base = base + landed[i, dx * 2 + dc - 1]
            own[i, dc] = base
        c = copy(own.at[i], near.at[i], s2.at[i], r2.at[i], 0, 2)
        c.start()
        nearby.append(c)
        sums.append(project(0, 0, own[i, 0]) + project(0, 1, own[i, 1]))
    pend += nearby

    for c in sm:
        c.wait_recv()
    block = small_out[ig]
    for d in range(1, ng):
        block = block + small_in[d - 1]
    small_sum[...] = block
    zx = []
    for d in range(1, nx):
        zx.append(copy(
            small_sum.at[0:SUB], zsum_in.at[d - 1], t3.at[d - 1], u3.at[d - 1], d, 0
        ))
        zx[-1].start()
    pend += zx

    far = []
    for i in range(chunks):
        nearby[i].wait_recv()
        total = sums[i] + project(1, 0, near[i, 0]) + project(1, 1, near[i, 1])
        far_out[i] = total[blk_b * SUB :]
        c = copy(far_out.at[i], far_in.at[i], s3.at[i], r3.at[i], 0, 4)
        c.start()
        far.append(c)
        sums[i] = total[: blk_b * SUB]
    pend += far

    for c in zx:
        c.wait_recv()
    zpart = small_sum[0:SUB]
    for d in range(1, nx):
        zpart = zpart + zsum_in[d - 1]
    zx_out[0:SUB] = zpart
    zx_out[SUB:] = small_sum[SUB:]
    gathered = []
    for d in range(1, ng):
        gathered.append(copy(zx_out, zx_in.at[d - 1], t4.at[d - 1], u4.at[d - 1], 0, d))
        gathered[-1].start()
    pend += gathered
    for c in fy:
        c.wait_recv()
    value = fy_out[...]
    for d in range(1, nx):
        value = value + fy_in[d - 1]
    out_y[...] = (value * (1.0 / math.sqrt(front * nx * depth)))[:, :RANK]

    scale = 1.0 / math.sqrt(front * nx * back * ng * depth)
    finals = []
    for i in range(chunks):
        far[i].wait_recv()
        high, low = split(sums[i] + far_in[i])
        value = (mm(high, phi_z) + mm(low, phi_z)) * scale
        done_out[i] = value.reshape(2, out_b * SUB, depth)
        c = copy(done_out.at[i, 1 - core], done_in.at[i], s4.at[i], r4.at[i], 0, 1)
        c.start()
        finals.append(c)
        mine = done_out[i, core]
        for b in range(out_b):
            out_core[pl.ds((i * 2 * SUB + core * SUB) * out_b + b, SUB, stride=out_b), :] = (
                mine[b * SUB : (b + 1) * SUB]
            )
    pend += finals

    for c in gathered:
        c.wait_recv()
    for c in sm:
        c.wait_send()
    for d in range(ng):
        block = zx_out[...] if d == 0 else zx_in[d - 1]
        small_out[dev_g(d)] = block
    scale_x = 1.0 / math.sqrt(back * ng * depth)
    scale_z = 1.0 / math.sqrt(front * nx * back * ng)
    for d in range(ng):
        out_x[d * per : (d + 1) * per, :] = small_out[d, SUB : SUB + per, :RANK] * scale_x
    whole = jnp.concatenate([small_out[d, 0:kper] for d in range(ng)], axis=0)
    out_z[...] = whole.T * scale_z

    for i in range(chunks):
        finals[i].wait_recv()
        other = done_in[i]
        for b in range(out_b):
            out_core[
                pl.ds((i * 2 * SUB + (1 - core) * SUB) * out_b + b, SUB, stride=out_b), :
            ] = other[b * SUB : (b + 1) * SUB]
    for c in pend:
        c.wait_send()


def fused_body(nx, ng, thermal_field, generator_keys, slab_top_offset):
    front, back, depth = thermal_field.shape
    nz = ng // 2
    blk_a = TARGET_RANK // nx
    chunks = blk_a // (2 * SUB)
    blk_b = TARGET_RANK // nz
    out_b = blk_b // 2
    f32 = jnp.float32
    vmem = pltpu.VMEM
    dma = pltpu.SemaphoreType.DMA
    peers = 2 * nx - 1
    scratch = [
        vmem((back, TARGET_RANK, depth), f32),
        vmem((chunks, peers, back, SUB, depth), f32),
        vmem((chunks, 2, back, SUB, depth), f32),
        vmem((chunks, 2, back, SUB, depth), f32),
        vmem((chunks, blk_b * SUB, depth), f32),
        vmem((chunks, blk_b * SUB, depth), f32),
        vmem((chunks, 2, out_b * SUB, depth), f32),
        vmem((chunks, out_b * SUB, depth), f32),
        vmem((2, 2, 2 * blk_b * SUB, back * SUB), jnp.bfloat16),
        vmem((ng, 2 * SUB, LANES), f32),
        vmem((ng - 1, 2 * SUB, LANES), f32),
        vmem((2 * SUB, LANES), f32),
        vmem((nx - 1, SUB, LANES), f32),
        vmem((2 * SUB, LANES), f32),
        vmem((ng - 1, 2 * SUB, LANES), f32),
        vmem((back, LANES), f32),
        vmem((nx - 1, back, LANES), f32),
        dma((chunks, peers)), dma((chunks, peers)),
        dma((chunks,)), dma((chunks,)),
        dma((chunks,)), dma((chunks,)),
        dma((chunks,)), dma((chunks,)),
        dma((nx - 1,)), dma((nx - 1,)),
        dma((ng - 1,)), dma((ng - 1,)),
        dma((nx - 1,)), dma((nx - 1,)),
        dma((ng - 1,)), dma((ng - 1,)),
    ]
    whole = pl.BlockSpec(memory_space=pltpu.VMEM)
    scalar = pl.BlockSpec(memory_space=pltpu.SMEM)
    fx, fy, fz, core = pl.pallas_call(
        functools.partial(kernel, (nx, ng, front, back, depth)),
        out_shape=(
            jax.ShapeDtypeStruct((front, RANK), f32),
            jax.ShapeDtypeStruct((back, RANK), f32),
            jax.ShapeDtypeStruct((depth, RANK), f32),
            jax.ShapeDtypeStruct((blk_a * out_b, depth), f32),
        ),
        in_specs=[scalar, scalar, whole],
        out_specs=(whole,) * 4,
        scratch_shapes=scratch,
        compiler_params=pltpu.CompilerParams(
            collective_id=0, has_side_effects=True, vmem_limit_bytes=40 * 2**20
        ),
    )(generator_keys, slab_top_offset, thermal_field.reshape(front * back, depth))
    return fx, fy, fz, core.reshape(blk_a, out_b, depth)


def suits(nx, ng):
    return nx == 4 and ng == 8


def solution(mesh):
    nx, ng = mesh.shape["gx"], mesh.shape["gy"]
    chosen = functools.partial(fused_body, nx, ng) if suits(nx, ng) else body
    placed = (P("gx", "gy", None), P(), P())
    return jax.shard_map(
        chosen,
        mesh=mesh,
        in_specs=placed,
        out_specs=(P("gx", None), P("gy", None), P(), P("gx", "gy", None)),
        check_vma=False,
    )
```

```python
import functools
import math

import jax
import jax.numpy as jnp
from jax import lax
from jax.experimental import pallas as pl
from jax.experimental.pallas import tpu as pltpu
from jax.sharding import PartitionSpec as P

RANK = 64
TARGET_RANK = 128


def random_signs(seed_value, cell_index, column_index):
    hashed = cell_index * 73856093 + column_index * 19349663 + seed_value * 83492791
    hashed = jnp.bitwise_xor(hashed, lax.shift_right_logical(hashed, jnp.full_like(hashed, 15)))
    hashed = hashed * 668265261
    hashed = jnp.bitwise_xor(hashed, lax.shift_right_logical(hashed, jnp.full_like(hashed, 13)))
    parity = jnp.bitwise_and(
        lax.shift_right_logical(hashed, jnp.full_like(hashed, 7)), jnp.full_like(hashed, 1)
    )
    return jnp.where(parity == 1, 1.0, -1.0).astype(jnp.float32)


def body(thermal_field, generator_keys, slab_top_offset):
    exact_matmul_mode = lax.Precision.HIGHEST
    front_length, back_length, vertical_layer = thermal_field.shape
    devices_first = lax.axis_size("gx")
    devices_second = lax.axis_size("gy")
    total_first = front_length * devices_first
    total_second = back_length * devices_second
    x_index = (lax.axis_index("gx") * front_length + jnp.arange(front_length, dtype=jnp.int32))[
        :, None
    ]
    y_index = (lax.axis_index("gy") * back_length + jnp.arange(back_length, dtype=jnp.int32))[
        :, None
    ]
    z_index = (slab_top_offset[0] + jnp.arange(vertical_layer, dtype=jnp.int32))[:, None]
    rank_cols = jnp.arange(RANK, dtype=jnp.int32)[None, :]
    core_cols = jnp.arange(TARGET_RANK, dtype=jnp.int32)[None, :]
    omega_x = random_signs(generator_keys[0], x_index, rank_cols)
    omega_y = random_signs(generator_keys[1], y_index, rank_cols)
    omega_z = random_signs(generator_keys[2], z_index, rank_cols)
    phi_xt = random_signs(generator_keys[3], x_index, core_cols).T
    phi_yt = random_signs(generator_keys[4], y_index, core_cols).T
    phi_z = random_signs(generator_keys[5], z_index, core_cols)
    unrolled_grid = thermal_field.reshape(front_length * back_length, vertical_layer)
    reduced = jnp.dot(unrolled_grid, omega_z, precision=exact_matmul_mode).reshape(
        front_length, back_length, RANK
    )
    partial_x = jnp.einsum("xyk,yk->xk", reduced, omega_y, precision=exact_matmul_mode)
    partial_y = jnp.einsum("xyk,xk->yk", reduced, omega_x, precision=exact_matmul_mode)
    khatri = (omega_x[:, None, :] * omega_y[None, :, :]).reshape(front_length * back_length, RANK)
    partial_z = jnp.einsum("pz,pk->zk", unrolled_grid, khatri, precision=exact_matmul_mode)
    summed_x, half_z = lax.psum((partial_x, partial_z), "gy")
    summed_y, summed_z = lax.psum((partial_y, half_z), "gx")
    factor_x = summed_x * (1.0 / math.sqrt(total_second * vertical_layer))
    factor_y = summed_y * (1.0 / math.sqrt(total_first * vertical_layer))
    factor_z = summed_z * (1.0 / math.sqrt(total_first * total_second))
    thermal_matrix = thermal_field.reshape(front_length, back_length * vertical_layer)
    chosen_entries = phi_xt
    reduced_first = lax.psum_scatter(
        jnp.dot(chosen_entries, thermal_matrix, precision=exact_matmul_mode),
        "gx",
        scatter_dimension=0,
        tiled=True,
    )
    reduced_first = reduced_first.reshape(-1, back_length, vertical_layer)
    chosen_entries = phi_yt
    middle = jnp.einsum("by,ayz->baz", chosen_entries, reduced_first, precision=exact_matmul_mode)
    swapped = lax.psum_scatter(
        jnp.einsum("baz,zc->bac", middle, phi_z, precision=exact_matmul_mode),
        "gy",
        scatter_dimension=0,
        tiled=True,
    )
    core_block = jnp.transpose(swapped, (1, 0, 2))
    core = core_block * (1.0 / math.sqrt(total_first * total_second * vertical_layer))
    return (factor_x, factor_y, factor_z, core)


SUB = 8
LANES = 128
MESH_ID = pl.DeviceIdType.MESH


def signs(seed_value, cell_index, column_index):
    hashed = cell_index * 73856093 + column_index * 19349663 + seed_value * 83492791
    hashed = hashed ^ lax.shift_right_logical(hashed, jnp.full_like(hashed, 15))
    hashed = hashed * 668265261
    hashed = hashed ^ lax.shift_right_logical(hashed, jnp.full_like(hashed, 13))
    return jnp.where((hashed & 128) != 0, 1.0, -1.0).astype(jnp.float32)


def iota(shape, axis):
    return lax.broadcasted_iota(jnp.int32, shape, axis)


def split(value):
    high = value.astype(jnp.bfloat16)
    low = (value - high.astype(jnp.float32)).astype(jnp.bfloat16)
    return high, low


def mm(left, right):
    return jnp.dot(left, right, preferred_element_type=jnp.float32)


def flip(index, bit):
    return index + bit - 2 * bit * ((index // bit) % 2)


def way_of(group, groups, core):
    if 2 * group + 1 == groups:
        return core
    return 0 if 2 * group < groups else 1


def step_x(ix, way, turn):
    low = flip(ix, 1)
    high = flip(ix, 2)
    first = low + (high - low) * way
    return first if turn == 0 else low + high - first


def kernel(
    dims,
    keys, top, field,
    out_x, out_y, out_z, out_core,
    raw_in, spread, landed, own, near, far_out, far_in, done_out, done_in, kron,
    small_out, small_in, small_sum, zsum_in, zx_out, zx_in, fy_out, fy_in,
    s0, r0, s5, r5, s1, r1, s2, r2, s3, r3, s4, r4, t1, u1, t2, u2, t3, u3, t4, u4,
):
    nx, ng, front, back, depth = dims
    nz = ng // 2
    blk_a = TARGET_RANK // nx
    chunks = blk_a // (2 * SUB)
    blk_b = TARGET_RANK // nz
    out_b = blk_b // 2
    ix = lax.axis_index("gx")
    ig = lax.axis_index("gy")
    iz, core = ig // 2, ig % 2

    def dev_x(d):
        r = ix
        for bit in (1, 2):
            if d & bit:
                r = flip(r, bit)
        return r

    def dev_g(d):
        r = ig
        for bit in (1, 2, 4):
            if d & bit:
                r = flip(r, bit)
        return r

    def copy(src, dst, send, recv, dx, dg):
        return pltpu.make_async_remote_copy(
            src_ref=src, dst_ref=dst, send_sem=send, recv_sem=recv,
            device_id=(dev_x(dx), dev_g(dg)), device_id_type=MESH_ID,
        )

    partners = [(dx, dc) for dx in range(nx) for dc in range(2) if dx or dc]
    partners += [(0, dg) for dg in range(2, ng)]
    barrier = pltpu.get_barrier_semaphore()
    for dx, dg in partners:
        pl.semaphore_signal(
            barrier, inc=1, device_id=(dev_x(dx), dev_g(dg)), device_id_type=MESH_ID
        )

    x0 = ix * front
    y0 = ig * back
    z0 = top[0]

    groups = back // SUB
    two_d = field.reshape(front * back, depth)

    pl.semaphore_wait(barrier, len(partners))
    raws = []
    for g in range(groups):
        way = way_of(g, groups, core)
        near_x = step_x(ix, way, 0)
        raws.append(pltpu.make_async_remote_copy(
            src_ref=field.at[:, g * SUB : (g + 1) * SUB, :], dst_ref=raw_in.at[g],
            send_sem=s0.at[g], recv_sem=r0.at[g],
            device_id=(near_x, ig), device_id_type=MESH_ID,
        ))
        raws[-1].start()
    pend = list(raws)

    x0 = ix * front
    y0 = ig * back
    z0 = top[0]
    rows = 2 * blk_a + RANK
    omega_yt = signs(keys[1], iota((RANK, back), 1) + y0, iota((RANK, back), 0))
    total_z = jnp.zeros((RANK, depth), jnp.float32)
    for g in range(groups):
        way = way_of(g, groups, core)
        row = iota((rows, 2 * front), 0)
        lane = iota((rows, 2 * front), 1)
        cell = jnp.where(lane >= front, lane - front, lane) + x0
        target = jnp.where(row < blk_a, ix * blk_a, step_x(ix, way, 1) * blk_a - blk_a) + row
        is_core = row < 2 * blk_a
        left = signs(
            jnp.where(is_core, keys[3], keys[0]),
            cell,
            jnp.where(is_core, target, row - 2 * blk_a),
        ).astype(jnp.bfloat16)
        for y in range(g * SUB, (g + 1) * SUB):
            high, low = split(two_d[pl.ds(y, front, stride=back), :])
            both = mm(left, jnp.concatenate([high, low], axis=0))
            spread[y] = both[: 2 * blk_a]
            total_z = total_z + both[2 * blk_a :] * omega_yt[:, y : y + 1]

    lane_z = iota((depth, LANES), 1)
    row_z = iota((depth, LANES), 0) + z0
    omega_z = signs(keys[2], row_z, lane_z).astype(jnp.bfloat16)
    high, low = split(two_d[...])
    reduced = (mm(high, omega_z) + mm(low, omega_z)).reshape(front, back, LANES)
    omega_y = signs(keys[1], iota((back, LANES), 0) + y0, iota((back, LANES), 1))
    part_y = jnp.zeros((back, LANES), jnp.float32)
    omega_x = signs(keys[0], iota((front, LANES), 0) + x0, iota((front, LANES), 1))
    part_x = jnp.sum(reduced * omega_y[None], axis=1)
    for x in range(front):
        part_y = part_y + reduced[x] * omega_x[x : x + 1]
    fy_out[...] = part_y
    per = front // ng
    kper = RANK // ng
    for d in range(ng):
        small_out[d, 0:kper] = total_z[d * kper : (d + 1) * kper]
        small_out[d, SUB : SUB + per] = part_x[d * per : (d + 1) * per]
    fy = []
    for d in range(1, nx):
        fy.append(copy(fy_out, fy_in.at[d - 1], t1.at[d - 1], u1.at[d - 1], d, 0))
        fy[-1].start()
    sm = []
    for d in range(1, ng):
        sm.append(copy(
            small_out.at[dev_g(d)], small_in.at[d - 1], t2.at[d - 1], u2.at[d - 1], 0, d
        ))
        sm[-1].start()
    pend += fy

    half = 2 * back * SUB
    for dst in range(2):
        for src in range(2):
            for dc in range(2):
                shape = (blk_b * SUB, back * SUB)
                row = iota(shape, 0)
                col = iota(shape, 1)
                chip_b = (flip(iz, 2) if dst else iz) * blk_b
                cell_y = dev_g(src * 2 + dc) * back
                value = signs(
                    keys[4],
                    lax.shift_right_logical(col, jnp.full_like(col, 3)) + cell_y,
                    lax.shift_right_logical(row, jnp.full_like(row, 3)) + chip_b,
                )
                value = jnp.where((row & 7) == (col & 7), value, 0.0)
                kron[src, dc, dst * blk_b * SUB : (dst + 1) * blk_b * SUB, :] = value.astype(
                    jnp.bfloat16
                )
    phi_z = signs(keys[5], row_z, lane_z).astype(jnp.bfloat16)

    def project(src, dc, block):
        high, low = split(block.reshape(back * SUB, depth))
        return mm(kron[src, dc], high) + mm(kron[src, dc], low)

    sends = [[] for _ in range(chunks)]

    def send_far(i, g):
        way = way_of(g, groups, core)
        for dc in (1, 0):
            start = blk_a + i * 2 * SUB + (dev_g(dc) % 2) * SUB
            sends[i].append(pltpu.make_async_remote_copy(
                src_ref=spread.at[g * SUB : (g + 1) * SUB, pl.ds(pl.multiple_of(start, SUB), SUB), :],
                dst_ref=landed.at[i, dc, g * SUB : (g + 1) * SUB],
                send_sem=s1.at[i, dc, g], recv_sem=r1.at[i, dc, g],
                device_id=(step_x(ix, way, 1), dev_g(dc)), device_id_type=MESH_ID,
            ))
            sends[i][-1].start()

    def send_core(i):
        start = pl.multiple_of(i * 2 * SUB + (1 - core) * SUB, SUB)
        sends[i].append(copy(
            spread.at[:, pl.ds(start, SUB), :], landed.at[i, 2],
            s5.at[i], r5.at[i], 0, 1,
        ))
        sends[i][-1].start()

    for g in range(groups):
        way = way_of(g, groups, core)
        shape = (2 * blk_a, 2 * front)
        row = iota(shape, 0)
        lane = iota(shape, 1)
        cell = jnp.where(lane >= front, lane - front, lane) + step_x(ix, way, 0) * front
        target = jnp.where(row < blk_a, ix * blk_a, step_x(ix, way, 1) * blk_a - blk_a) + row
        left = signs(keys[3], cell, target).astype(jnp.bfloat16)
        raws[g].wait_recv()
        flat = raw_in.at[g].reshape(front * SUB, depth)
        for y in range(SUB):
            high, low = split(flat[pl.ds(y, front, stride=SUB), :])
            spread[g * SUB + y] += mm(left, jnp.concatenate([high, low], axis=0))
        send_far(0, g)
    send_core(0)
    for i in range(1, chunks):
        for g in range(groups):
            send_far(i, g)
        send_core(i)
    pend += sum(sends, [])

    nearby = []
    sums = []
    for i in range(chunks):
        for c in sends[i]:
            c.wait_recv()
        start = pl.multiple_of(i * 2 * SUB + core * SUB, SUB)
        own[i, 0] = spread[:, pl.ds(start, SUB), :] + landed[i, 0]
        own[i, 1] = landed[i, 2] + landed[i, 1]
        c = copy(own.at[i], near.at[i], s2.at[i], r2.at[i], 0, 2)
        c.start()
        nearby.append(c)
        sums.append(project(0, 0, own[i, 0]) + project(0, 1, own[i, 1]))
    pend += nearby

    for c in sm:
        c.wait_recv()
    block = small_out[ig]
    for d in range(1, ng):
        block = block + small_in[d - 1]
    small_sum[...] = block
    zx = []
    for d in range(1, nx):
        zx.append(copy(
            small_sum.at[0:SUB], zsum_in.at[d - 1], t3.at[d - 1], u3.at[d - 1], d, 0
        ))
        zx[-1].start()
    pend += zx

    far = []
    for i in range(chunks):
        nearby[i].wait_recv()
        total = sums[i] + project(1, 0, near[i, 0]) + project(1, 1, near[i, 1])
        far_out[i] = total[blk_b * SUB :]
        c = copy(far_out.at[i], far_in.at[i], s3.at[i], r3.at[i], 0, 4)
        c.start()
        far.append(c)
        sums[i] = total[: blk_b * SUB]
    pend += far

    for c in zx:
        c.wait_recv()
    zpart = small_sum[0:SUB]
    for d in range(1, nx):
        zpart = zpart + zsum_in[d - 1]
    zx_out[0:SUB] = zpart
    zx_out[SUB:] = small_sum[SUB:]
    gathered = []
    for d in range(1, ng):
        gathered.append(copy(zx_out, zx_in.at[d - 1], t4.at[d - 1], u4.at[d - 1], 0, d))
        gathered[-1].start()
    pend += gathered
    for c in fy:
        c.wait_recv()
    value = fy_out[...]
    for d in range(1, nx):
        value = value + fy_in[d - 1]
    out_y[...] = (value * (1.0 / math.sqrt(front * nx * depth)))[:, :RANK]

    scale = 1.0 / math.sqrt(front * nx * back * ng * depth)
    finals = []
    for i in range(chunks):
        far[i].wait_recv()
        high, low = split(sums[i] + far_in[i])
        value = (mm(high, phi_z) + mm(low, phi_z)) * scale
        done_out[i] = value.reshape(2, out_b * SUB, depth)
        c = copy(done_out.at[i, 1 - core], done_in.at[i], s4.at[i], r4.at[i], 0, 1)
        c.start()
        finals.append(c)
        mine = done_out[i, core]
        for b in range(out_b):
            out_core[pl.ds((i * 2 * SUB + core * SUB) * out_b + b, SUB, stride=out_b), :] = (
                mine[b * SUB : (b + 1) * SUB]
            )
    pend += finals

    for c in gathered:
        c.wait_recv()
    for c in sm:
        c.wait_send()
    for d in range(ng):
        block = zx_out[...] if d == 0 else zx_in[d - 1]
        small_out[dev_g(d)] = block
    scale_x = 1.0 / math.sqrt(back * ng * depth)
    scale_z = 1.0 / math.sqrt(front * nx * back * ng)
    for d in range(ng):
        out_x[d * per : (d + 1) * per, :] = small_out[d, SUB : SUB + per, :RANK] * scale_x
    whole = jnp.concatenate([small_out[d, 0:kper] for d in range(ng)], axis=0)
    out_z[...] = whole.T * scale_z

    for i in range(chunks):
        finals[i].wait_recv()
        other = done_in[i]
        for b in range(out_b):
            out_core[
                pl.ds((i * 2 * SUB + (1 - core) * SUB) * out_b + b, SUB, stride=out_b), :
            ] = other[b * SUB : (b + 1) * SUB]
    for c in pend:
        c.wait_send()


def fused_body(nx, ng, thermal_field, generator_keys, slab_top_offset):
    front, back, depth = thermal_field.shape
    nz = ng // 2
    blk_a = TARGET_RANK // nx
    chunks = blk_a // (2 * SUB)
    blk_b = TARGET_RANK // nz
    out_b = blk_b // 2
    f32 = jnp.float32
    vmem = pltpu.VMEM
    dma = pltpu.SemaphoreType.DMA
    groups = back // SUB
    scratch = [
        vmem((groups, front, SUB, depth), f32),
        vmem((back, 2 * blk_a, depth), f32),
        vmem((chunks, 3, back, SUB, depth), f32),
        vmem((chunks, 2, back, SUB, depth), f32),
        vmem((chunks, 2, back, SUB, depth), f32),
        vmem((chunks, blk_b * SUB, depth), f32),
        vmem((chunks, blk_b * SUB, depth), f32),
        vmem((chunks, 2, out_b * SUB, depth), f32),
        vmem((chunks, out_b * SUB, depth), f32),
        vmem((2, 2, 2 * blk_b * SUB, back * SUB), jnp.bfloat16),
        vmem((ng, 2 * SUB, LANES), f32),
        vmem((ng - 1, 2 * SUB, LANES), f32),
        vmem((2 * SUB, LANES), f32),
        vmem((nx - 1, SUB, LANES), f32),
        vmem((2 * SUB, LANES), f32),
        vmem((ng - 1, 2 * SUB, LANES), f32),
        vmem((back, LANES), f32),
        vmem((nx - 1, back, LANES), f32),
        dma((groups,)), dma((groups,)),
        dma((chunks,)), dma((chunks,)),
        dma((chunks, 2, groups)), dma((chunks, 2, groups)),
        dma((chunks,)), dma((chunks,)),
        dma((chunks,)), dma((chunks,)),
        dma((chunks,)), dma((chunks,)),
        dma((nx - 1,)), dma((nx - 1,)),
        dma((ng - 1,)), dma((ng - 1,)),
        dma((nx - 1,)), dma((nx - 1,)),
        dma((ng - 1,)), dma((ng - 1,)),
    ]
    whole = pl.BlockSpec(memory_space=pltpu.VMEM)
    scalar = pl.BlockSpec(memory_space=pltpu.SMEM)
    fx, fy, fz, core = pl.pallas_call(
        functools.partial(kernel, (nx, ng, front, back, depth)),
        out_shape=(
            jax.ShapeDtypeStruct((front, RANK), f32),
            jax.ShapeDtypeStruct((back, RANK), f32),
            jax.ShapeDtypeStruct((depth, RANK), f32),
            jax.ShapeDtypeStruct((blk_a * out_b, depth), f32),
        ),
        in_specs=[scalar, scalar, whole],
        out_specs=(whole,) * 4,
        scratch_shapes=scratch,
        compiler_params=pltpu.CompilerParams(
            collective_id=0, has_side_effects=True, vmem_limit_bytes=40 * 2**20
        ),
    )(generator_keys, slab_top_offset, thermal_field)
    return fx, fy, fz, core.reshape(blk_a, out_b, depth)


def suits(nx, ng):
    return nx == 4 and ng == 8


def solution(mesh):
    nx, ng = mesh.shape["gx"], mesh.shape["gy"]
    chosen = functools.partial(fused_body, nx, ng) if suits(nx, ng) else body
    placed = (P("gx", "gy", None), P(), P())
    return jax.shard_map(
        chosen,
        mesh=mesh,
        in_specs=placed,
        out_specs=(P("gx", None), P("gy", None), P(), P("gx", "gy", None)),
        check_vma=False,
    )
```

```python
import functools
import math

import jax
import jax.numpy as jnp
from jax import lax
from jax.experimental import pallas as pl
from jax.experimental.pallas import tpu as pltpu
from jax.sharding import PartitionSpec as P

RANK = 64
TARGET_RANK = 128


def random_signs(seed_value, cell_index, column_index):
    hashed = cell_index * 73856093 + column_index * 19349663 + seed_value * 83492791
    hashed = jnp.bitwise_xor(hashed, lax.shift_right_logical(hashed, jnp.full_like(hashed, 15)))
    hashed = hashed * 668265261
    hashed = jnp.bitwise_xor(hashed, lax.shift_right_logical(hashed, jnp.full_like(hashed, 13)))
    parity = jnp.bitwise_and(
        lax.shift_right_logical(hashed, jnp.full_like(hashed, 7)), jnp.full_like(hashed, 1)
    )
    return jnp.where(parity == 1, 1.0, -1.0).astype(jnp.float32)


def body(thermal_field, generator_keys, slab_top_offset):
    exact_matmul_mode = lax.Precision.HIGHEST
    front_length, back_length, vertical_layer = thermal_field.shape
    devices_first = lax.axis_size("gx")
    devices_second = lax.axis_size("gy")
    total_first = front_length * devices_first
    total_second = back_length * devices_second
    x_index = (lax.axis_index("gx") * front_length + jnp.arange(front_length, dtype=jnp.int32))[
        :, None
    ]
    y_index = (lax.axis_index("gy") * back_length + jnp.arange(back_length, dtype=jnp.int32))[
        :, None
    ]
    z_index = (slab_top_offset[0] + jnp.arange(vertical_layer, dtype=jnp.int32))[:, None]
    rank_cols = jnp.arange(RANK, dtype=jnp.int32)[None, :]
    core_cols = jnp.arange(TARGET_RANK, dtype=jnp.int32)[None, :]
    omega_x = random_signs(generator_keys[0], x_index, rank_cols)
    omega_y = random_signs(generator_keys[1], y_index, rank_cols)
    omega_z = random_signs(generator_keys[2], z_index, rank_cols)
    phi_xt = random_signs(generator_keys[3], x_index, core_cols).T
    phi_yt = random_signs(generator_keys[4], y_index, core_cols).T
    phi_z = random_signs(generator_keys[5], z_index, core_cols)
    unrolled_grid = thermal_field.reshape(front_length * back_length, vertical_layer)
    reduced = jnp.dot(unrolled_grid, omega_z, precision=exact_matmul_mode).reshape(
        front_length, back_length, RANK
    )
    partial_x = jnp.einsum("xyk,yk->xk", reduced, omega_y, precision=exact_matmul_mode)
    partial_y = jnp.einsum("xyk,xk->yk", reduced, omega_x, precision=exact_matmul_mode)
    khatri = (omega_x[:, None, :] * omega_y[None, :, :]).reshape(front_length * back_length, RANK)
    partial_z = jnp.einsum("pz,pk->zk", unrolled_grid, khatri, precision=exact_matmul_mode)
    summed_x, half_z = lax.psum((partial_x, partial_z), "gy")
    summed_y, summed_z = lax.psum((partial_y, half_z), "gx")
    factor_x = summed_x * (1.0 / math.sqrt(total_second * vertical_layer))
    factor_y = summed_y * (1.0 / math.sqrt(total_first * vertical_layer))
    factor_z = summed_z * (1.0 / math.sqrt(total_first * total_second))
    thermal_matrix = thermal_field.reshape(front_length, back_length * vertical_layer)
    chosen_entries = phi_xt
    reduced_first = lax.psum_scatter(
        jnp.dot(chosen_entries, thermal_matrix, precision=exact_matmul_mode),
        "gx",
        scatter_dimension=0,
        tiled=True,
    )
    reduced_first = reduced_first.reshape(-1, back_length, vertical_layer)
    chosen_entries = phi_yt
    middle = jnp.einsum("by,ayz->baz", chosen_entries, reduced_first, precision=exact_matmul_mode)
    swapped = lax.psum_scatter(
        jnp.einsum("baz,zc->bac", middle, phi_z, precision=exact_matmul_mode),
        "gy",
        scatter_dimension=0,
        tiled=True,
    )
    core_block = jnp.transpose(swapped, (1, 0, 2))
    core = core_block * (1.0 / math.sqrt(total_first * total_second * vertical_layer))
    return (factor_x, factor_y, factor_z, core)


SUB = 8
LANES = 128
MESH_ID = pl.DeviceIdType.MESH


def signs(seed_value, cell_index, column_index):
    hashed = cell_index * 73856093 + column_index * 19349663 + seed_value * 83492791
    hashed = hashed ^ lax.shift_right_logical(hashed, jnp.full_like(hashed, 15))
    hashed = hashed * 668265261
    hashed = hashed ^ lax.shift_right_logical(hashed, jnp.full_like(hashed, 13))
    return jnp.where((hashed & 128) != 0, 1.0, -1.0).astype(jnp.float32)


def iota(shape, axis):
    return lax.broadcasted_iota(jnp.int32, shape, axis)


def split(value):
    high = value.astype(jnp.bfloat16)
    low = (value - high.astype(jnp.float32)).astype(jnp.bfloat16)
    return high, low


def mm(left, right):
    return jnp.dot(left, right, preferred_element_type=jnp.float32)


def flip(index, bit):
    return index + bit - 2 * bit * ((index // bit) % 2)


def way_of(group, groups, core):
    if 2 * group + 1 == groups:
        return core
    return 0 if 2 * group < groups else 1


def step_x(ix, way, turn):
    low = flip(ix, 1)
    high = flip(ix, 2)
    first = low + (high - low) * way
    return first if turn == 0 else low + high - first


def kernel(
    dims,
    keys, top, field_in,
    out_x, out_y, out_z, out_core,
    field, load_sem, raw_out, raw_in, spread, landed, own, near, far_out, far_in, done_out, done_in, kron,
    small_out, small_in, small_sum, zsum_in, zx_out, zx_in, fy_out, fy_in,
    s0, r0, s5, r5, s1, r1, s2, r2, s3, r3, s4, r4, t1, u1, t2, u2, t3, u3, t4, u4,
):
    nx, ng, front, back, depth = dims
    nz = ng // 2
    blk_a = TARGET_RANK // nx
    chunks = blk_a // (2 * SUB)
    blk_b = TARGET_RANK // nz
    out_b = blk_b // 2
    ix = lax.axis_index("gx")
    ig = lax.axis_index("gy")
    iz, core = ig // 2, ig % 2

    def dev_x(d):
        r = ix
        for bit in (1, 2):
            if d & bit:
                r = flip(r, bit)
        return r

    def dev_g(d):
        r = ig
        for bit in (1, 2, 4):
            if d & bit:
                r = flip(r, bit)
        return r

    def copy(src, dst, send, recv, dx, dg):
        return pltpu.make_async_remote_copy(
            src_ref=src, dst_ref=dst, send_sem=send, recv_sem=recv,
            device_id=(dev_x(dx), dev_g(dg)), device_id_type=MESH_ID,
        )

    partners = [(dx, dc) for dx in range(nx) for dc in range(2) if dx or dc]
    partners += [(0, dg) for dg in range(2, ng)]
    barrier = pltpu.get_barrier_semaphore()
    for dx, dg in partners:
        pl.semaphore_signal(
            barrier, inc=1, device_id=(dev_x(dx), dev_g(dg)), device_id_type=MESH_ID
        )

    x0 = ix * front
    y0 = ig * back
    z0 = top[0]

    groups = back // SUB
    fold = front // 2
    deep = depth // 2
    load = pltpu.make_async_copy(field_in, field, load_sem)
    load.start()
    two_d = field.reshape(front * back, depth)
    x0 = ix * front
    y0 = ig * back
    z0 = top[0]
    lower = iota((fold, SUB, depth), 2) < deep
    raws = []
    load.wait()
    for h in range(2):
        for g in range(groups):
            here = field[0:fold, g * SUB : (g + 1) * SUB, :]
            there = field[fold:front, g * SUB : (g + 1) * SUB, :]
            if h == 0:
                raw_out[h, g] = jnp.where(lower, here, pltpu.roll(there, deep, 2))
            else:
                raw_out[h, g] = jnp.where(lower, pltpu.roll(here, deep, 2), there)
    pl.semaphore_wait(barrier, len(partners))
    for h in range(2):
        for g in range(groups):
            near_x = step_x(ix, way_of(g, groups, core), 0)
            raws.append(pltpu.make_async_remote_copy(
                src_ref=raw_out.at[h, g], dst_ref=raw_in.at[h, g],
                send_sem=s0.at[h, g], recv_sem=r0.at[h, g],
                device_id=(near_x, ig), device_id_type=MESH_ID,
            ))
            raws[-1].start()
    pend = list(raws)

    pairs = blk_a // 2

    def weights(base, far_x):
        shape = (4 * pairs, 4 * fold)
        row = iota(shape, 0)
        lane = iota(shape, 1)
        lane = jnp.where(lane >= front, lane - front, lane)
        second = row >= 2 * pairs
        row = jnp.where(second, row - 2 * pairs, row)
        swapped = jnp.where(lane >= fold, lane - fold, lane + fold)
        cell = jnp.where(second, swapped, lane) + base
        target = jnp.where(row < pairs, ix * blk_a, far_x * blk_a - pairs) + row
        target = jnp.where(second, target + pairs, target)
        return signs(keys[3], cell, target).astype(jnp.bfloat16)

    lower_row = iota((2 * pairs, depth), 1) < deep

    def contract(left, packed):
        both = jnp.concatenate([packed, pltpu.roll(packed, deep, 1)], axis=0)
        high, low = split(both)
        out = mm(left, jnp.concatenate([high, low], axis=0))
        return jnp.where(lower_row, out[: 2 * pairs], out[2 * pairs :])

    for g in range(groups):
        way = way_of(g, groups, core)
        left = weights(x0, step_x(ix, way, 1))
        for h in range(2):
            flat = raw_out.at[h, g].reshape(fold * SUB, depth)
            for y in range(SUB):
                spread[h, g * SUB + y] = contract(left, flat[pl.ds(y, fold, stride=SUB), :])
    lane = iota((RANK, 2 * front), 1)
    left = signs(
        keys[0], jnp.where(lane >= front, lane - front, lane) + x0, iota((RANK, 2 * front), 0)
    ).astype(jnp.bfloat16)
    omega_yt = signs(keys[1], iota((RANK, back), 1) + y0, iota((RANK, back), 0))
    total_z = jnp.zeros((RANK, depth), jnp.float32)
    for y in range(back):
        high, low = split(two_d[pl.ds(y, front, stride=back), :])
        both = mm(left, jnp.concatenate([high, low], axis=0))
        total_z = total_z + both * omega_yt[:, y : y + 1]

    lane_z = iota((depth, LANES), 1)
    row_z = iota((depth, LANES), 0) + z0
    omega_z = signs(keys[2], row_z, lane_z).astype(jnp.bfloat16)
    high, low = split(two_d[...])
    reduced = (mm(high, omega_z) + mm(low, omega_z)).reshape(front, back, LANES)
    omega_y = signs(keys[1], iota((back, LANES), 0) + y0, iota((back, LANES), 1))
    part_y = jnp.zeros((back, LANES), jnp.float32)
    omega_x = signs(keys[0], iota((front, LANES), 0) + x0, iota((front, LANES), 1))
    part_x = jnp.sum(reduced * omega_y[None], axis=1)
    for x in range(front):
        part_y = part_y + reduced[x] * omega_x[x : x + 1]
    fy_out[...] = part_y
    per = front // ng
    kper = RANK // ng
    for d in range(ng):
        small_out[d, 0:kper] = total_z[d * kper : (d + 1) * kper]
        small_out[d, SUB : SUB + per] = part_x[d * per : (d + 1) * per]
    fy = []
    for d in range(1, nx):
        fy.append(copy(fy_out, fy_in.at[d - 1], t1.at[d - 1], u1.at[d - 1], d, 0))
        fy[-1].start()
    sm = []
    for d in range(1, ng):
        sm.append(copy(
            small_out.at[dev_g(d)], small_in.at[d - 1], t2.at[d - 1], u2.at[d - 1], 0, d
        ))
        sm[-1].start()
    pend += fy

    half = 2 * back * SUB
    for dst in range(2):
        for src in range(2):
            for dc in range(2):
                shape = (blk_b * SUB, back * SUB)
                row = iota(shape, 0)
                col = iota(shape, 1)
                chip_b = (flip(iz, 2) if dst else iz) * blk_b
                cell_y = dev_g(src * 2 + dc) * back
                value = signs(
                    keys[4],
                    lax.shift_right_logical(col, jnp.full_like(col, 3)) + cell_y,
                    lax.shift_right_logical(row, jnp.full_like(row, 3)) + chip_b,
                )
                value = jnp.where((row & 7) == (col & 7), value, 0.0)
                kron[src, dc, dst * blk_b * SUB : (dst + 1) * blk_b * SUB, :] = value.astype(
                    jnp.bfloat16
                )
    row = iota((depth, 2 * LANES), 0)
    col = iota((depth, 2 * LANES), 1)
    same = (row >= deep) == (col >= LANES)
    row = jnp.where(row >= deep, row - deep, row) + z0
    col = jnp.where(col >= LANES, col - LANES, col)
    phi_z = [
        jnp.where(same, signs(keys[5], row + h * deep, col), 0.0).astype(jnp.bfloat16)
        for h in range(2)
    ]

    def project(src, dc, block):
        high, low = split(block.reshape(back * SUB, depth))
        return mm(kron[src, dc], high) + mm(kron[src, dc], low)

    sends = [[] for _ in range(chunks)]
    lefts = []
    for g in range(groups):
        way = way_of(g, groups, core)
        lefts.append(weights(step_x(ix, way, 0) * front, step_x(ix, way, 1)))
    for i in range(chunks):
        for g in range(groups):
            raws[i * groups + g].wait_recv()
            flat = raw_in.at[i, g].reshape(fold * SUB, depth)
            for y in range(SUB):
                spread[i, g * SUB + y] += contract(
                    lefts[g], flat[pl.ds(y, fold, stride=SUB), :]
                )
            for dc in (1, 0):
                start = pl.multiple_of(pairs + (dev_g(dc) % 2) * SUB, SUB)
                sends[i].append(pltpu.make_async_remote_copy(
                    src_ref=spread.at[i, g * SUB : (g + 1) * SUB, pl.ds(start, SUB), :],
                    dst_ref=landed.at[i, dc, g * SUB : (g + 1) * SUB],
                    send_sem=s1.at[i, dc, g], recv_sem=r1.at[i, dc, g],
                    device_id=(step_x(ix, way_of(g, groups, core), 1), dev_g(dc)),
                    device_id_type=MESH_ID,
                ))
                sends[i][-1].start()
        start = pl.multiple_of((1 - core) * SUB, SUB)
        sends[i].append(copy(
            spread.at[i, :, pl.ds(start, SUB), :], landed.at[i, 2], s5.at[i], r5.at[i], 0, 1
        ))
        sends[i][-1].start()
    pend += sum(sends, [])

    nearby = []
    sums = []
    for i in range(chunks):
        for c in sends[i]:
            c.wait_recv()
        own[i, 0] = spread[i, :, pl.ds(pl.multiple_of(core * SUB, SUB), SUB), :] + landed[i, 0]
        own[i, 1] = landed[i, 2] + landed[i, 1]
        c = copy(own.at[i], near.at[i], s2.at[i], r2.at[i], 0, 2)
        c.start()
        nearby.append(c)
        sums.append(project(0, 0, own[i, 0]) + project(0, 1, own[i, 1]))
    pend += nearby

    for c in sm:
        c.wait_recv()
    block = small_out[ig]
    for d in range(1, ng):
        block = block + small_in[d - 1]
    small_sum[...] = block
    zx = []
    for d in range(1, nx):
        zx.append(copy(
            small_sum.at[0:SUB], zsum_in.at[d - 1], t3.at[d - 1], u3.at[d - 1], d, 0
        ))
        zx[-1].start()
    pend += zx

    far = []
    for i in range(chunks):
        nearby[i].wait_recv()
        total = sums[i] + project(1, 0, near[i, 0]) + project(1, 1, near[i, 1])
        far_out[i] = total[blk_b * SUB :]
        c = copy(far_out.at[i], far_in.at[i], s3.at[i], r3.at[i], 0, 4)
        c.start()
        far.append(c)
        sums[i] = total[: blk_b * SUB]
    pend += far

    for c in zx:
        c.wait_recv()
    zpart = small_sum[0:SUB]
    for d in range(1, nx):
        zpart = zpart + zsum_in[d - 1]
    zx_out[0:SUB] = zpart
    zx_out[SUB:] = small_sum[SUB:]
    gathered = []
    for d in range(1, ng):
        gathered.append(copy(zx_out, zx_in.at[d - 1], t4.at[d - 1], u4.at[d - 1], 0, d))
        gathered[-1].start()
    pend += gathered
    for c in fy:
        c.wait_recv()
    value = fy_out[...]
    for d in range(1, nx):
        value = value + fy_in[d - 1]
    out_y[...] = (value * (1.0 / math.sqrt(front * nx * depth)))[:, :RANK]

    scale = 1.0 / math.sqrt(front * nx * back * ng * depth)
    finals = []
    mine = 0.0

    def last(i, block):
        high, low = split(block)
        return mm(high, phi_z[i]) + mm(low, phi_z[i])

    def put(which, value):
        value = value * scale
        for i in range(chunks):
            for b in range(out_b):
                out_core[pl.ds((i * pairs + which * SUB) * out_b + b, SUB, stride=out_b), :] = (
                    value[b * SUB : (b + 1) * SUB, i * LANES : (i + 1) * LANES]
                )

    for i in range(chunks):
        far[i].wait_recv()
        done_out[i] = (sums[i] + far_in[i]).reshape(2, out_b * SUB, depth)
        c = copy(done_out.at[i, 1 - core], done_in.at[i], s4.at[i], r4.at[i], 0, 1)
        c.start()
        finals.append(c)
        mine = mine + last(i, done_out[i, core])
    put(core, mine)
    pend += finals

    for c in gathered:
        c.wait_recv()
    for c in sm:
        c.wait_send()
    for d in range(ng):
        block = zx_out[...] if d == 0 else zx_in[d - 1]
        small_out[dev_g(d)] = block
    scale_x = 1.0 / math.sqrt(back * ng * depth)
    scale_z = 1.0 / math.sqrt(front * nx * back * ng)
    for d in range(ng):
        out_x[d * per : (d + 1) * per, :] = small_out[d, SUB : SUB + per, :RANK] * scale_x
    whole = jnp.concatenate([small_out[d, 0:kper] for d in range(ng)], axis=0)
    out_z[...] = whole.T * scale_z

    other = 0.0
    for i in range(chunks):
        finals[i].wait_recv()
        other = other + last(i, done_in[i])
    put(1 - core, other)
    for c in pend:
        c.wait_send()


def fused_body(nx, ng, thermal_field, generator_keys, slab_top_offset):
    front, back, depth = thermal_field.shape
    nz = ng // 2
    blk_a = TARGET_RANK // nx
    chunks = blk_a // (2 * SUB)
    blk_b = TARGET_RANK // nz
    out_b = blk_b // 2
    f32 = jnp.float32
    vmem = pltpu.VMEM
    dma = pltpu.SemaphoreType.DMA
    groups = back // SUB
    scratch = [
        vmem((front, back, depth), f32),
        dma(()),
        vmem((2, groups, front // 2, SUB, depth), f32),
        vmem((2, groups, front // 2, SUB, depth), f32),
        vmem((2, back, blk_a, depth), f32),
        vmem((chunks, 3, back, SUB, depth), f32),
        vmem((chunks, 2, back, SUB, depth), f32),
        vmem((chunks, 2, back, SUB, depth), f32),
        vmem((chunks, blk_b * SUB, depth), f32),
        vmem((chunks, blk_b * SUB, depth), f32),
        vmem((chunks, 2, out_b * SUB, depth), f32),
        vmem((chunks, out_b * SUB, depth), f32),
        vmem((2, 2, 2 * blk_b * SUB, back * SUB), jnp.bfloat16),
        vmem((ng, 2 * SUB, LANES), f32),
        vmem((ng - 1, 2 * SUB, LANES), f32),
        vmem((2 * SUB, LANES), f32),
        vmem((nx - 1, SUB, LANES), f32),
        vmem((2 * SUB, LANES), f32),
        vmem((ng - 1, 2 * SUB, LANES), f32),
        vmem((back, LANES), f32),
        vmem((nx - 1, back, LANES), f32),
        dma((2, groups)), dma((2, groups)),
        dma((chunks,)), dma((chunks,)),
        dma((chunks, 2, groups)), dma((chunks, 2, groups)),
        dma((chunks,)), dma((chunks,)),
        dma((chunks,)), dma((chunks,)),
        dma((chunks,)), dma((chunks,)),
        dma((nx - 1,)), dma((nx - 1,)),
        dma((ng - 1,)), dma((ng - 1,)),
        dma((nx - 1,)), dma((nx - 1,)),
        dma((ng - 1,)), dma((ng - 1,)),
    ]
    whole = pl.BlockSpec(memory_space=pltpu.VMEM)
    scalar = pl.BlockSpec(memory_space=pltpu.SMEM)
    fx, fy, fz, core = pl.pallas_call(
        functools.partial(kernel, (nx, ng, front, back, depth)),
        out_shape=(
            jax.ShapeDtypeStruct((front, RANK), f32),
            jax.ShapeDtypeStruct((back, RANK), f32),
            jax.ShapeDtypeStruct((depth, RANK), f32),
            jax.ShapeDtypeStruct((blk_a * out_b, depth), f32),
        ),
        in_specs=[scalar, scalar, pl.BlockSpec(memory_space=pl.ANY)],
        out_specs=(whole,) * 4,
        scratch_shapes=scratch,
        compiler_params=pltpu.CompilerParams(
            collective_id=0, has_side_effects=True, vmem_limit_bytes=40 * 2**20
        ),
    )(generator_keys, slab_top_offset, thermal_field)
    return fx, fy, fz, core.reshape(blk_a, out_b, depth)


def suits(nx, ng):
    return nx == 4 and ng == 8


def solution(mesh):
    nx, ng = mesh.shape["gx"], mesh.shape["gy"]
    chosen = functools.partial(fused_body, nx, ng) if suits(nx, ng) else body
    placed = (P("gx", "gy", None), P(), P())
    return jax.shard_map(
        chosen,
        mesh=mesh,
        in_specs=placed,
        out_specs=(P("gx", None), P("gy", None), P(), P("gx", "gy", None)),
        check_vma=False,
    )
```

```python
import functools
import math

import jax
import jax.numpy as jnp
from jax import lax
from jax.experimental import pallas as pl
from jax.experimental.pallas import tpu as pltpu
from jax.sharding import PartitionSpec as P

RANK = 64
TARGET_RANK = 128


def random_signs(seed_value, cell_index, column_index):
    hashed = cell_index * 73856093 + column_index * 19349663 + seed_value * 83492791
    hashed = jnp.bitwise_xor(hashed, lax.shift_right_logical(hashed, jnp.full_like(hashed, 15)))
    hashed = hashed * 668265261
    hashed = jnp.bitwise_xor(hashed, lax.shift_right_logical(hashed, jnp.full_like(hashed, 13)))
    parity = jnp.bitwise_and(
        lax.shift_right_logical(hashed, jnp.full_like(hashed, 7)), jnp.full_like(hashed, 1)
    )
    return jnp.where(parity == 1, 1.0, -1.0).astype(jnp.float32)


def body(thermal_field, generator_keys, slab_top_offset):
    exact_matmul_mode = lax.Precision.HIGHEST
    front_length, back_length, vertical_layer = thermal_field.shape
    devices_first = lax.axis_size("gx")
    devices_second = lax.axis_size("gy")
    total_first = front_length * devices_first
    total_second = back_length * devices_second
    x_index = (lax.axis_index("gx") * front_length + jnp.arange(front_length, dtype=jnp.int32))[
        :, None
    ]
    y_index = (lax.axis_index("gy") * back_length + jnp.arange(back_length, dtype=jnp.int32))[
        :, None
    ]
    z_index = (slab_top_offset[0] + jnp.arange(vertical_layer, dtype=jnp.int32))[:, None]
    rank_cols = jnp.arange(RANK, dtype=jnp.int32)[None, :]
    core_cols = jnp.arange(TARGET_RANK, dtype=jnp.int32)[None, :]
    omega_x = random_signs(generator_keys[0], x_index, rank_cols)
    omega_y = random_signs(generator_keys[1], y_index, rank_cols)
    omega_z = random_signs(generator_keys[2], z_index, rank_cols)
    phi_xt = random_signs(generator_keys[3], x_index, core_cols).T
    phi_yt = random_signs(generator_keys[4], y_index, core_cols).T
    phi_z = random_signs(generator_keys[5], z_index, core_cols)
    unrolled_grid = thermal_field.reshape(front_length * back_length, vertical_layer)
    reduced = jnp.dot(unrolled_grid, omega_z, precision=exact_matmul_mode).reshape(
        front_length, back_length, RANK
    )
    partial_x = jnp.einsum("xyk,yk->xk", reduced, omega_y, precision=exact_matmul_mode)
    partial_y = jnp.einsum("xyk,xk->yk", reduced, omega_x, precision=exact_matmul_mode)
    khatri = (omega_x[:, None, :] * omega_y[None, :, :]).reshape(front_length * back_length, RANK)
    partial_z = jnp.einsum("pz,pk->zk", unrolled_grid, khatri, precision=exact_matmul_mode)
    summed_x, half_z = lax.psum((partial_x, partial_z), "gy")
    summed_y, summed_z = lax.psum((partial_y, half_z), "gx")
    factor_x = summed_x * (1.0 / math.sqrt(total_second * vertical_layer))
    factor_y = summed_y * (1.0 / math.sqrt(total_first * vertical_layer))
    factor_z = summed_z * (1.0 / math.sqrt(total_first * total_second))
    thermal_matrix = thermal_field.reshape(front_length, back_length * vertical_layer)
    chosen_entries = phi_xt
    reduced_first = lax.psum_scatter(
        jnp.dot(chosen_entries, thermal_matrix, precision=exact_matmul_mode),
        "gx",
        scatter_dimension=0,
        tiled=True,
    )
    reduced_first = reduced_first.reshape(-1, back_length, vertical_layer)
    chosen_entries = phi_yt
    middle = jnp.einsum("by,ayz->baz", chosen_entries, reduced_first, precision=exact_matmul_mode)
    swapped = lax.psum_scatter(
        jnp.einsum("baz,zc->bac", middle, phi_z, precision=exact_matmul_mode),
        "gy",
        scatter_dimension=0,
        tiled=True,
    )
    core_block = jnp.transpose(swapped, (1, 0, 2))
    core = core_block * (1.0 / math.sqrt(total_first * total_second * vertical_layer))
    return (factor_x, factor_y, factor_z, core)


SUB = 8
LANES = 128
MESH_ID = pl.DeviceIdType.MESH


def signs(seed_value, cell_index, column_index):
    hashed = cell_index * 73856093 + column_index * 19349663 + seed_value * 83492791
    hashed = hashed ^ lax.shift_right_logical(hashed, jnp.full_like(hashed, 15))
    hashed = hashed * 668265261
    hashed = hashed ^ lax.shift_right_logical(hashed, jnp.full_like(hashed, 13))
    return jnp.where((hashed & 128) != 0, 1.0, -1.0).astype(jnp.float32)


def iota(shape, axis):
    return lax.broadcasted_iota(jnp.int32, shape, axis)


def split(value):
    high = value.astype(jnp.bfloat16)
    low = (value - high.astype(jnp.float32)).astype(jnp.bfloat16)
    return high, low


def mm(left, right):
    return jnp.dot(left, right, preferred_element_type=jnp.float32)


def flip(index, bit):
    return index + bit - 2 * bit * ((index // bit) % 2)


def way_of(group, groups, core):
    if 2 * group + 1 == groups:
        return core
    return 0 if 2 * group < groups else 1


def step_x(ix, way, turn):
    low = flip(ix, 1)
    high = flip(ix, 2)
    first = low + (high - low) * way
    return first if turn == 0 else low + high - first


def kernel(
    dims,
    keys, top, field_in,
    out_x, out_y, out_z, out_core,
    field, load_sem, raw_out, raw_in, spread, landed, own, near, far_out, far_in, done_out, done_in, kron,
    small_out, small_in, small_sum, zsum_in, zx_out, zx_in, fy_out, fy_in,
    s0, r0, s5, r5, s1, r1, s2, r2, s3, r3, s4, r4, t1, u1, t2, u2, t3, u3, t4, u4,
):
    nx, ng, front, back, depth = dims
    nz = ng // 2
    blk_a = TARGET_RANK // nx
    chunks = blk_a // (2 * SUB)
    blk_b = TARGET_RANK // nz
    out_b = blk_b // 2
    ix = lax.axis_index("gx")
    ig = lax.axis_index("gy")
    iz, core = ig // 2, ig % 2

    def dev_x(d):
        r = ix
        for bit in (1, 2):
            if d & bit:
                r = flip(r, bit)
        return r

    def dev_g(d):
        r = ig
        for bit in (1, 2, 4):
            if d & bit:
                r = flip(r, bit)
        return r

    def copy(src, dst, send, recv, dx, dg):
        return pltpu.make_async_remote_copy(
            src_ref=src, dst_ref=dst, send_sem=send, recv_sem=recv,
            device_id=(dev_x(dx), dev_g(dg)), device_id_type=MESH_ID,
        )

    partners = [(dx, dc) for dx in range(nx) for dc in range(2) if dx or dc]
    partners += [(0, dg) for dg in range(2, ng)]
    barrier = pltpu.get_barrier_semaphore()
    for dx, dg in partners:
        pl.semaphore_signal(
            barrier, inc=1, device_id=(dev_x(dx), dev_g(dg)), device_id_type=MESH_ID
        )

    x0 = ix * front
    y0 = ig * back
    z0 = top[0]

    groups = back // SUB
    fold = front // 2
    deep = depth // 2
    load = pltpu.make_async_copy(field_in, field, load_sem)
    load.start()
    two_d = field.reshape(front * back, depth)
    x0 = ix * front
    y0 = ig * back
    z0 = top[0]
    lower = iota((fold, SUB, depth), 2) < deep
    raws = []
    load.wait()
    for h in range(2):
        for g in range(groups):
            here = field[0:fold, g * SUB : (g + 1) * SUB, :]
            there = field[fold:front, g * SUB : (g + 1) * SUB, :]
            if h == 0:
                raw_out[h, g] = jnp.where(lower, here, pltpu.roll(there, deep, 2))
            else:
                raw_out[h, g] = jnp.where(lower, pltpu.roll(here, deep, 2), there)
    pl.semaphore_wait(barrier, len(partners))
    for h in range(2):
        for g in range(groups):
            near_x = step_x(ix, way_of(g, groups, core), 0)
            raws.append(pltpu.make_async_remote_copy(
                src_ref=raw_out.at[h, g], dst_ref=raw_in.at[h, g],
                send_sem=s0.at[h, g], recv_sem=r0.at[h, g],
                device_id=(near_x, ig), device_id_type=MESH_ID,
            ))
            raws[-1].start()
    pend = list(raws)

    pairs = blk_a // 2

    def weights(base, far_x):
        shape = (4 * pairs, 4 * fold)
        row = iota(shape, 0)
        lane = iota(shape, 1)
        lane = jnp.where(lane >= front, lane - front, lane)
        second = row >= 2 * pairs
        row = jnp.where(second, row - 2 * pairs, row)
        swapped = jnp.where(lane >= fold, lane - fold, lane + fold)
        cell = jnp.where(second, swapped, lane) + base
        target = jnp.where(row < pairs, ix * blk_a, far_x * blk_a - pairs) + row
        target = jnp.where(second, target + pairs, target)
        return signs(keys[3], cell, target).astype(jnp.bfloat16)

    lower_row = iota((2 * pairs, depth), 1) < deep

    def contract(left, packed):
        both = jnp.concatenate([packed, pltpu.roll(packed, deep, 1)], axis=0)
        high, low = split(both)
        out = mm(left, jnp.concatenate([high, low], axis=0))
        return jnp.where(lower_row, out[: 2 * pairs], out[2 * pairs :])

    sends = [[] for _ in range(chunks)]
    lefts = []
    owns = []
    for g in range(groups):
        way = way_of(g, groups, core)
        owns.append(weights(x0, step_x(ix, way, 1)))
        lefts.append(weights(step_x(ix, way, 0) * front, step_x(ix, way, 1)))
    for i in range(chunks):
        for g in range(groups):
            flat = raw_out.at[i, g].reshape(fold * SUB, depth)
            for y in range(SUB):
                spread[i, g * SUB + y] = contract(owns[g], flat[pl.ds(y, fold, stride=SUB), :])
        for g in range(groups):
            raws[i * groups + g].wait_recv()
            flat = raw_in.at[i, g].reshape(fold * SUB, depth)
            for y in range(SUB):
                spread[i, g * SUB + y] += contract(
                    lefts[g], flat[pl.ds(y, fold, stride=SUB), :]
                )
            for dc in (1, 0):
                start = pl.multiple_of(pairs + (dev_g(dc) % 2) * SUB, SUB)
                sends[i].append(pltpu.make_async_remote_copy(
                    src_ref=spread.at[i, g * SUB : (g + 1) * SUB, pl.ds(start, SUB), :],
                    dst_ref=landed.at[i, dc, g * SUB : (g + 1) * SUB],
                    send_sem=s1.at[i, dc, g], recv_sem=r1.at[i, dc, g],
                    device_id=(step_x(ix, way_of(g, groups, core), 1), dev_g(dc)),
                    device_id_type=MESH_ID,
                ))
                sends[i][-1].start()
        start = pl.multiple_of((1 - core) * SUB, SUB)
        sends[i].append(copy(
            spread.at[i, :, pl.ds(start, SUB), :], landed.at[i, 2], s5.at[i], r5.at[i], 0, 1
        ))
        sends[i][-1].start()
    pend += sum(sends, [])

    lane = iota((RANK, 2 * front), 1)
    left = signs(
        keys[0], jnp.where(lane >= front, lane - front, lane) + x0, iota((RANK, 2 * front), 0)
    ).astype(jnp.bfloat16)
    omega_yt = signs(keys[1], iota((RANK, back), 1) + y0, iota((RANK, back), 0))
    total_z = jnp.zeros((RANK, depth), jnp.float32)
    for y in range(back):
        high, low = split(two_d[pl.ds(y, front, stride=back), :])
        both = mm(left, jnp.concatenate([high, low], axis=0))
        total_z = total_z + both * omega_yt[:, y : y + 1]

    lane_z = iota((depth, LANES), 1)
    row_z = iota((depth, LANES), 0) + z0
    omega_z = signs(keys[2], row_z, lane_z).astype(jnp.bfloat16)
    high, low = split(two_d[...])
    reduced = (mm(high, omega_z) + mm(low, omega_z)).reshape(front, back, LANES)
    omega_y = signs(keys[1], iota((back, LANES), 0) + y0, iota((back, LANES), 1))
    part_y = jnp.zeros((back, LANES), jnp.float32)
    omega_x = signs(keys[0], iota((front, LANES), 0) + x0, iota((front, LANES), 1))
    part_x = jnp.sum(reduced * omega_y[None], axis=1)
    for x in range(front):
        part_y = part_y + reduced[x] * omega_x[x : x + 1]
    fy_out[...] = part_y
    per = front // ng
    kper = RANK // ng
    for d in range(ng):
        small_out[d, 0:kper] = total_z[d * kper : (d + 1) * kper]
        small_out[d, SUB : SUB + per] = part_x[d * per : (d + 1) * per]
    fy = []
    for d in range(1, nx):
        fy.append(copy(fy_out, fy_in.at[d - 1], t1.at[d - 1], u1.at[d - 1], d, 0))
        fy[-1].start()
    sm = []
    for d in range(1, ng):
        sm.append(copy(
            small_out.at[dev_g(d)], small_in.at[d - 1], t2.at[d - 1], u2.at[d - 1], 0, d
        ))
        sm[-1].start()
    pend += fy

    half = 2 * back * SUB
    for dst in range(2):
        for src in range(2):
            for dc in range(2):
                shape = (blk_b * SUB, back * SUB)
                row = iota(shape, 0)
                col = iota(shape, 1)
                chip_b = (flip(iz, 2) if dst else iz) * blk_b
                cell_y = dev_g(src * 2 + dc) * back
                value = signs(
                    keys[4],
                    lax.shift_right_logical(col, jnp.full_like(col, 3)) + cell_y,
                    lax.shift_right_logical(row, jnp.full_like(row, 3)) + chip_b,
                )
                value = jnp.where((row & 7) == (col & 7), value, 0.0)
                kron[src, dc, dst * blk_b * SUB : (dst + 1) * blk_b * SUB, :] = value.astype(
                    jnp.bfloat16
                )
    row = iota((depth, 2 * LANES), 0)
    col = iota((depth, 2 * LANES), 1)
    same = (row >= deep) == (col >= LANES)
    row = jnp.where(row >= deep, row - deep, row) + z0
    col = jnp.where(col >= LANES, col - LANES, col)
    phi_z = [
        jnp.where(same, signs(keys[5], row + h * deep, col), 0.0).astype(jnp.bfloat16)
        for h in range(2)
    ]

    def project(src, dc, block):
        high, low = split(block.reshape(back * SUB, depth))
        return mm(kron[src, dc], high) + mm(kron[src, dc], low)

    nearby = []
    sums = []
    for i in range(chunks):
        for c in sends[i]:
            c.wait_recv()
        own[i, 0] = spread[i, :, pl.ds(pl.multiple_of(core * SUB, SUB), SUB), :] + landed[i, 0]
        own[i, 1] = landed[i, 2] + landed[i, 1]
        c = copy(own.at[i], near.at[i], s2.at[i], r2.at[i], 0, 2)
        c.start()
        nearby.append(c)
        sums.append(project(0, 0, own[i, 0]) + project(0, 1, own[i, 1]))
    pend += nearby

    for c in sm:
        c.wait_recv()
    block = small_out[ig]
    for d in range(1, ng):
        block = block + small_in[d - 1]
    small_sum[...] = block
    zx = []
    for d in range(1, nx):
        zx.append(copy(
            small_sum.at[0:SUB], zsum_in.at[d - 1], t3.at[d - 1], u3.at[d - 1], d, 0
        ))
        zx[-1].start()
    pend += zx

    far = []
    for i in range(chunks):
        nearby[i].wait_recv()
        total = sums[i] + project(1, 0, near[i, 0]) + project(1, 1, near[i, 1])
        far_out[i] = total[blk_b * SUB :]
        c = copy(far_out.at[i], far_in.at[i], s3.at[i], r3.at[i], 0, 4)
        c.start()
        far.append(c)
        sums[i] = total[: blk_b * SUB]
    pend += far

    for c in zx:
        c.wait_recv()
    zpart = small_sum[0:SUB]
    for d in range(1, nx):
        zpart = zpart + zsum_in[d - 1]
    zx_out[0:SUB] = zpart
    zx_out[SUB:] = small_sum[SUB:]
    gathered = []
    for d in range(1, ng):
        gathered.append(copy(zx_out, zx_in.at[d - 1], t4.at[d - 1], u4.at[d - 1], 0, d))
        gathered[-1].start()
    pend += gathered
    for c in fy:
        c.wait_recv()
    value = fy_out[...]
    for d in range(1, nx):
        value = value + fy_in[d - 1]
    out_y[...] = (value * (1.0 / math.sqrt(front * nx * depth)))[:, :RANK]

    scale = 1.0 / math.sqrt(front * nx * back * ng * depth)
    finals = []
    mine = 0.0

    def last(i, block):
        high, low = split(block)
        return mm(high, phi_z[i]) + mm(low, phi_z[i])

    def put(which, value):
        value = value * scale
        for i in range(chunks):
            for b in range(out_b):
                out_core[pl.ds((i * pairs + which * SUB) * out_b + b, SUB, stride=out_b), :] = (
                    value[b * SUB : (b + 1) * SUB, i * LANES : (i + 1) * LANES]
                )

    for i in range(chunks):
        far[i].wait_recv()
        done_out[i] = (sums[i] + far_in[i]).reshape(2, out_b * SUB, depth)
        c = copy(done_out.at[i, 1 - core], done_in.at[i], s4.at[i], r4.at[i], 0, 1)
        c.start()
        finals.append(c)
        mine = mine + last(i, done_out[i, core])
    put(core, mine)
    pend += finals

    for c in gathered:
        c.wait_recv()
    for c in sm:
        c.wait_send()
    for d in range(ng):
        block = zx_out[...] if d == 0 else zx_in[d - 1]
        small_out[dev_g(d)] = block
    scale_x = 1.0 / math.sqrt(back * ng * depth)
    scale_z = 1.0 / math.sqrt(front * nx * back * ng)
    for d in range(ng):
        out_x[d * per : (d + 1) * per, :] = small_out[d, SUB : SUB + per, :RANK] * scale_x
    whole = jnp.concatenate([small_out[d, 0:kper] for d in range(ng)], axis=0)
    out_z[...] = whole.T * scale_z

    other = 0.0
    for i in range(chunks):
        finals[i].wait_recv()
        other = other + last(i, done_in[i])
    put(1 - core, other)
    for c in pend:
        c.wait_send()


def fused_body(nx, ng, thermal_field, generator_keys, slab_top_offset):
    front, back, depth = thermal_field.shape
    nz = ng // 2
    blk_a = TARGET_RANK // nx
    chunks = blk_a // (2 * SUB)
    blk_b = TARGET_RANK // nz
    out_b = blk_b // 2
    f32 = jnp.float32
    vmem = pltpu.VMEM
    dma = pltpu.SemaphoreType.DMA
    groups = back // SUB
    scratch = [
        vmem((front, back, depth), f32),
        dma(()),
        vmem((2, groups, front // 2, SUB, depth), f32),
        vmem((2, groups, front // 2, SUB, depth), f32),
        vmem((2, back, blk_a, depth), f32),
        vmem((chunks, 3, back, SUB, depth), f32),
        vmem((chunks, 2, back, SUB, depth), f32),
        vmem((chunks, 2, back, SUB, depth), f32),
        vmem((chunks, blk_b * SUB, depth), f32),
        vmem((chunks, blk_b * SUB, depth), f32),
        vmem((chunks, 2, out_b * SUB, depth), f32),
        vmem((chunks, out_b * SUB, depth), f32),
        vmem((2, 2, 2 * blk_b * SUB, back * SUB), jnp.bfloat16),
        vmem((ng, 2 * SUB, LANES), f32),
        vmem((ng - 1, 2 * SUB, LANES), f32),
        vmem((2 * SUB, LANES), f32),
        vmem((nx - 1, SUB, LANES), f32),
        vmem((2 * SUB, LANES), f32),
        vmem((ng - 1, 2 * SUB, LANES), f32),
        vmem((back, LANES), f32),
        vmem((nx - 1, back, LANES), f32),
        dma((2, groups)), dma((2, groups)),
        dma((chunks,)), dma((chunks,)),
        dma((chunks, 2, groups)), dma((chunks, 2, groups)),
        dma((chunks,)), dma((chunks,)),
        dma((chunks,)), dma((chunks,)),
        dma((chunks,)), dma((chunks,)),
        dma((nx - 1,)), dma((nx - 1,)),
        dma((ng - 1,)), dma((ng - 1,)),
        dma((nx - 1,)), dma((nx - 1,)),
        dma((ng - 1,)), dma((ng - 1,)),
    ]
    whole = pl.BlockSpec(memory_space=pltpu.VMEM)
    scalar = pl.BlockSpec(memory_space=pltpu.SMEM)
    fx, fy, fz, core = pl.pallas_call(
        functools.partial(kernel, (nx, ng, front, back, depth)),
        out_shape=(
            jax.ShapeDtypeStruct((front, RANK), f32),
            jax.ShapeDtypeStruct((back, RANK), f32),
            jax.ShapeDtypeStruct((depth, RANK), f32),
            jax.ShapeDtypeStruct((blk_a * out_b, depth), f32),
        ),
        in_specs=[scalar, scalar, pl.BlockSpec(memory_space=pl.ANY)],
        out_specs=(whole,) * 4,
        scratch_shapes=scratch,
        compiler_params=pltpu.CompilerParams(
            collective_id=0, has_side_effects=True, vmem_limit_bytes=40 * 2**20
        ),
    )(generator_keys, slab_top_offset, thermal_field)
    return fx, fy, fz, core.reshape(blk_a, out_b, depth)


def suits(nx, ng):
    return nx == 4 and ng == 8


def solution(mesh):
    nx, ng = mesh.shape["gx"], mesh.shape["gy"]
    chosen = functools.partial(fused_body, nx, ng) if suits(nx, ng) else body
    placed = (P("gx", "gy", None), P(), P())
    return jax.shard_map(
        chosen,
        mesh=mesh,
        in_specs=placed,
        out_specs=(P("gx", None), P("gy", None), P(), P("gx", "gy", None)),
        check_vma=False,
    )
```
